32 devices in a mesh: dp: 4 (over y, x), ctx: 8 (over z, core).
Axes of the slice: x: 2, y: 2, z: 4, core: 2. Of those that a mesh axis runs over, the one named last changes fastest.
Arguments:
- hidden_in: bfloat16 [4, 1024, 768], P('dp', 'ctx'), may hold values from -6 to 6
- segment_ids: int32 [4, 1024], P('dp', 'ctx'), may hold values from 0 to 7, never falling along the last dimension, each value on 1 to 512 neighbouring positions
- grad_out: float32 [4, 1024, 768], P('dp', 'ctx'), may hold values from -6 to 6
- qkv_weight: bfloat16 [1, 768, 2304], P(None, ('dp', 'ctx')), may hold values from -0.21875 to 0.21875
- qv_bias: bfloat16 [1, 1536], P(None, ('dp', 'ctx')), may hold values from -3 to 3
- proj_weight: bfloat16 [1, 768, 768], P(None, ('dp', 'ctx')), may hold values from -0.875 to 0.875
- proj_bias: bfloat16 [1, 768], P(None, ('dp', 'ctx')), may hold values from -3 to 3
- first_gain: bfloat16 [1, 768], P(None, ('dp', 'ctx')), may hold values from 0.5 to 1.5
- first_shift: bfloat16 [1, 768], P(None, ('dp', 'ctx')), may hold values from -3 to 3
- up_weight: bfloat16 [1, 768, 3072], P(None, ('dp', 'ctx')), may hold values from -0.21875 to 0.21875
- up_bias: bfloat16 [1, 3072], P(None, ('dp', 'ctx')), may hold values from -3 to 3
- down_weight: bfloat16 [1, 3072, 768], P(None, ('dp', 'ctx')), may hold values from -0.109375 to 0.109375
- down_bias: bfloat16 [1, 768], P(None, ('dp', 'ctx')), may hold values from -3 to 3
- second_gain: bfloat16 [1, 768], P(None, ('dp', 'ctx')), may hold values from 0.5 to 1.5
- second_shift: bfloat16 [1, 768], P(None, ('dp', 'ctx')), may hold values from -3 to 3
Outputs:
- hidden_out: float32 [4, 1024, 768], P('dp', 'ctx')
- grad_in: float32 [4, 1024, 768], P('dp', 'ctx')
- qkv_weight_grad: float32 [1, 768, 2304], P(None, ('dp', 'ctx'))
- qv_bias_grad: float32 [1, 1536], P(None, ('dp', 'ctx'))
- proj_weight_grad: float32 [1, 768, 768], P(None, ('dp', 'ctx'))
- proj_bias_grad: float32 [1, 768], P(None, ('dp', 'ctx'))
- first_gain_grad: float32 [1, 768], P(None, ('dp', 'ctx'))
- first_shift_grad: float32 [1, 768], P(None, ('dp', 'ctx'))
- up_weight_grad: float32 [1, 768, 3072], P(None, ('dp', 'ctx'))
- up_bias_grad: float32 [1, 3072], P(None, ('dp', 'ctx'))
- down_weight_grad: float32 [1, 3072, 768], P(None, ('dp', 'ctx'))
- down_bias_grad: float32 [1, 768], P(None, ('dp', 'ctx'))
- second_gain_grad: float32 [1, 768], P(None, ('dp', 'ctx'))
- second_shift_grad: float32 [1, 768], P(None, ('dp', 'ctx'))
The draws below stay inside these ranges and needn't reach their ends.
Inputs may be any that keep to these rules, and one draw needn't show every extreme that they name: `segment_ids`: along each sequence the document numbers never fall; every document holds 1 to 512 positions and some document holds exactly 512.
All inputs are finite; a program needn't handle non-finite values.
Results may differ from the reference program's by a relative error of at most 0.013.
Values may be sent and summed in bfloat16 or wider, within the bound.
A program may use at most 128 MiB of HBM per device.

```python
import math
import jax
import jax.numpy as jnp
import numpy as np
from jax import lax

D = 768
HEADS = 12
HEAD_DIM = 64
FF = 3072
LAYERS = 1
SEQ = 1024
BATCH = 4


def levels(own_key, shape, pieces, smallest, top_value):
    level = 1.0
    for axis_at, blocks in pieces:
        draws = jax.random.uniform(jax.random.fold_in(jax.random.fold_in(own_key, 6), axis_at), (blocks,), jnp.float32, smallest / len(pieces), top_value / len(pieces))
        level = level * jnp.repeat(jnp.exp(draws), shape[axis_at] // blocks).reshape((-1,) + (1,) * (len(shape) - 1 - axis_at))
    return level


def profile(number_of, total, reach, slope):
    loads = [(1 << 20) // math.isqrt(grade ** slope) + 1 for grade in range(2, number_of + 1)]
    spare, given = total - reach - (number_of - 1), [1] * (number_of - 1)
    while spare > 0:
        free = [i for i in range(number_of - 1) if given[i] < reach]
        pool, remaining = sum([loads[i] for i in free]), spare
        for i in free:
            extra = min(reach - given[i], max(1, remaining * loads[i] // pool), spare)
            given[i] = given[i] + extra
            spare = spare - extra
    return np.array([reach] + given)


def uneven_parts(rng, count, total, most, slope):
    if count == 2:
        one = jax.random.randint(rng, (), max(1, total - most), min(most, total - 1) + 1)
        return jnp.stack([one, total - one])
    tallies = jnp.asarray(profile(count, total, most, slope), jnp.int32)
    twos = (count - 1) // 2
    source_of, receiver = tallies[1:1 + 2 * twos:2], tallies[2:2 + 2 * twos:2]
    slack = jnp.minimum(source_of - 1, most - receiver)
    moved = jax.random.randint(jax.random.fold_in(rng, 1), (twos,), 0, 1 << 20) % (slack + 1)
    tallies = tallies.at[1:1 + 2 * twos:2].set(source_of - moved).at[2:2 + 2 * twos:2].set(receiver + moved)
    return tallies[jax.random.permutation(jax.random.fold_in(rng, 2), count)]


def gaussian(key, shape, scale, limit, pieces=(), held_as=jnp.bfloat16):
    values = scale * jax.random.normal(key, shape, jnp.float32)
    if pieces:
        values = values * levels(key, shape, pieces, -0.22, 0.18)
    return jnp.clip(values, -limit, limit).astype(held_as)


def setup_inputs(seed: int = 0) -> dict:
    splits = jax.random.split(jax.random.key(seed), 16)
    hidden_in = gaussian(splits[0], (BATCH, SEQ, D), 1.0, 6.0, ((0, 4), (1, 8)))
    segment_ids = jax.vmap(lambda own: jnp.searchsorted(jnp.cumsum(uneven_parts(own, 8, SEQ, SEQ // 2, 2)), jnp.arange(SEQ), side="right"))(jax.random.split(splits[1], BATCH)).reshape((BATCH, SEQ)).astype(jnp.int32)
    grad_out = gaussian(splits[2], (BATCH, SEQ, D), 1.0, 6.0, ((0, 4), (1, 8)), jnp.float32)
    qkv_weight = gaussian(splits[3], (LAYERS, D, 3 * D), D ** -0.5, 0.21875, ((1, 32),))
    qv_bias = gaussian(splits[4], (LAYERS, 2 * D), 0.5, 3.0, ((1, 32),))
    proj_weight = gaussian(splits[5], (LAYERS, D, D), (D // 16) ** -0.5, 0.875, ((1, 32),))
    proj_bias = gaussian(splits[6], (LAYERS, D), 0.5, 3.0, ((1, 32),))
    first_gain = jnp.clip(1.0 + 0.1 * jax.random.normal(splits[7], (LAYERS, D), jnp.float32), 0.5, 1.5).astype(jnp.bfloat16)
    first_shift = gaussian(splits[8], (LAYERS, D), 0.5, 3.0, ((1, 32),))
    up_weight = gaussian(splits[9], (LAYERS, D, FF), D ** -0.5, 0.21875, ((1, 32),))
    up_bias = gaussian(splits[10], (LAYERS, FF), 0.5, 3.0, ((1, 32),))
    down_weight = gaussian(splits[11], (LAYERS, FF, D), FF ** -0.5, 0.109375, ((1, 32),))
    down_bias = gaussian(splits[12], (LAYERS, D), 0.5, 3.0, ((1, 32),))
    second_gain = jnp.clip(1.0 + 0.1 * jax.random.normal(splits[13], (LAYERS, D), jnp.float32), 0.5, 1.5).astype(jnp.bfloat16)
    second_shift = gaussian(splits[14], (LAYERS, D), 0.5, 3.0, ((1, 32),))
    return {"hidden_in": hidden_in, "segment_ids": segment_ids, "grad_out": grad_out, "qkv_weight": qkv_weight, "qv_bias": qv_bias, "proj_weight": proj_weight, "proj_bias": proj_bias, "first_gain": first_gain, "first_shift": first_shift, "up_weight": up_weight, "up_bias": up_bias, "down_weight": down_weight, "down_bias": down_bias, "second_gain": second_gain, "second_shift": second_shift}


def rounded(value):
    return lax.optimization_barrier(value.astype(jnp.bfloat16))

def layer_norm(resid, gain, shift):
    center = resid - lax.optimization_barrier(jnp.mean(resid, axis=-1, keepdims=True))
    variance = lax.optimization_barrier(jnp.mean(center * center, axis=-1, keepdims=True))
    return center * lax.rsqrt(variance + 1e-12) * gain + shift

def gelu_value(before):
    return before * 0.5 * (1.0 + lax.erf(before * (1.0 / math.sqrt(2.0))))

def gelu_slope(before):
    cumulative = 0.5 * (1.0 + lax.erf(before * (1.0 / math.sqrt(2.0))))
    density = jnp.exp(-0.5 * before * before) * (1.0 / math.sqrt(2.0 * math.pi))
    return cumulative + before * density

def scores_of(query_rows, key_rows, seg_ids):
    logits = jnp.einsum('qhd,khd->hqk', query_rows.astype(jnp.float32), key_rows.astype(jnp.float32))
    logits = logits * (1.0 / math.sqrt(HEAD_DIM))
    same = (seg_ids[:, None] == seg_ids[None, :])[None]
    return jnp.where(same, logits, -1e+30)

def attend_forward(query_rows, key_rows, value_rows, seg_ids):
    scores = scores_of(query_rows, key_rows, seg_ids)
    log_total = jnp.log(lax.optimization_barrier(jnp.sum(jnp.exp(scores), axis=-1, keepdims=True)))
    attn_weights = rounded(jnp.exp(scores - log_total))
    mixed = jnp.einsum('hqk,khd->qhd', attn_weights.astype(jnp.float32), value_rows.astype(jnp.float32))
    return (rounded(mixed), log_total)

def attend_backward(query_rows, key_rows, value_rows, seg_ids, log_total, grad_context):
    scores = scores_of(query_rows, key_rows, seg_ids)
    attn_weights = rounded(jnp.exp(scores - log_total)).astype(jnp.float32)
    grad_weights = jnp.einsum('qhd,khd->hqk', grad_context.astype(jnp.float32), value_rows.astype(jnp.float32))
    inner = lax.optimization_barrier(jnp.sum(attn_weights * grad_weights, axis=-1, keepdims=True))
    grad_scores = rounded(attn_weights * (grad_weights - inner) * (1.0 / math.sqrt(HEAD_DIM))).astype(jnp.float32)
    grad_query = jnp.einsum('hqk,khd->qhd', grad_scores, key_rows.astype(jnp.float32))
    grad_key = jnp.einsum('hqk,qhd->khd', grad_scores, query_rows.astype(jnp.float32))
    grad_value = jnp.einsum('hqk,qhd->khd', attn_weights, grad_context.astype(jnp.float32))
    return (grad_query, grad_key, grad_value)

def layer_forward(lowered, resid, seg_ids, params):
    qkv_w, qv_b, proj_w, proj_b, gain_a, shift_a, up_w, up_b, down_w, down_b, gain_b, shift_b = params
    width = qkv_w.shape[0]
    mixed_in = jnp.dot(lowered, qkv_w, preferred_element_type=jnp.float32)
    query_rows = rounded(mixed_in[:, :width] + qv_b[:width].astype(jnp.float32)).reshape(-1, HEADS, HEAD_DIM)
    key_rows = rounded(mixed_in[:, width:2 * width]).reshape(-1, HEADS, HEAD_DIM)
    value_rows = rounded(mixed_in[:, 2 * width:] + qv_b[width:].astype(jnp.float32)).reshape(-1, HEADS, HEAD_DIM)
    mixed, log_total = attend_forward(query_rows, key_rows, value_rows, seg_ids)
    context = mixed.reshape(-1, width)
    first_sum = resid + jnp.dot(context, proj_w, preferred_element_type=jnp.float32) + proj_b.astype(jnp.float32)
    normed = layer_norm(first_sum, gain_a.astype(jnp.float32), shift_a.astype(jnp.float32))
    normed_low = rounded(normed)
    before = jnp.dot(normed_low, up_w, preferred_element_type=jnp.float32) + up_b.astype(jnp.float32)
    activated = rounded(gelu_value(before))
    second_sum = normed + jnp.dot(activated, down_w, preferred_element_type=jnp.float32) + down_b.astype(jnp.float32)
    result = layer_norm(second_sum, gain_b.astype(jnp.float32), shift_b.astype(jnp.float32))
    record = (lowered, query_rows, key_rows, value_rows, log_total, context, first_sum, normed_low, before, activated, second_sum)
    return (record, result)

def layer_backward(record, upstream, seg_ids, params):
    qkv_w, qv_b, proj_w, proj_b, gain_a, shift_a, up_w, up_b, down_w, down_b, gain_b, shift_b = params
    lowered, query_rows, key_rows, value_rows, log_total, context, first_sum, normed_low, before, activated, second_sum = record
    width = qkv_w.shape[0]
    unused, second_back = jax.vjp(layer_norm, second_sum, gain_b.astype(jnp.float32), shift_b.astype(jnp.float32))
    grad_second, grad_gain_b, grad_shift_b = second_back(upstream)
    grad_second_low = rounded(grad_second)
    grad_down_w = jnp.dot(activated.T, grad_second_low, preferred_element_type=jnp.float32)
    grad_down_b = lax.optimization_barrier(jnp.sum(grad_second, axis=0))
    grad_before = jnp.dot(grad_second_low, down_w.T, preferred_element_type=jnp.float32) * gelu_slope(before)
    grad_up_b = lax.optimization_barrier(jnp.sum(grad_before, axis=0))
    grad_before_low = rounded(grad_before)
    grad_up_w = jnp.dot(normed_low.T, grad_before_low, preferred_element_type=jnp.float32)
    grad_normed = grad_second + jnp.dot(grad_before_low, up_w.T, preferred_element_type=jnp.float32)
    unused_two, first_back = jax.vjp(layer_norm, first_sum, gain_a.astype(jnp.float32), shift_a.astype(jnp.float32))
    grad_first, grad_gain_a, grad_shift_a = first_back(grad_normed)
    grad_first_low = rounded(grad_first)
    grad_proj_w = jnp.dot(context.T, grad_first_low, preferred_element_type=jnp.float32)
    grad_proj_b = lax.optimization_barrier(jnp.sum(grad_first, axis=0))
    grad_context = rounded(jnp.dot(grad_first_low, proj_w.T, preferred_element_type=jnp.float32)).reshape(-1, HEADS, HEAD_DIM)
    grad_query, grad_key, grad_value = attend_backward(query_rows, key_rows, value_rows, seg_ids, log_total, grad_context)
    grad_query = grad_query.reshape(-1, width)
    grad_key = grad_key.reshape(-1, width)
    grad_value = grad_value.reshape(-1, width)
    grad_qv_b = jnp.concatenate([lax.optimization_barrier(jnp.sum(grad_query, axis=0)), lax.optimization_barrier(jnp.sum(grad_value, axis=0))])
    grad_qkv = rounded(jnp.concatenate([grad_query, grad_key, grad_value], axis=1))
    grad_qkv_w = jnp.dot(lowered.T, grad_qkv, preferred_element_type=jnp.float32)
    grad_below = grad_first + jnp.dot(grad_qkv, qkv_w.T, preferred_element_type=jnp.float32)
    grads = (grad_qkv_w, grad_qv_b, grad_proj_w, grad_proj_b, grad_gain_a, grad_shift_a, grad_up_w, grad_up_b, grad_down_w, grad_down_b, grad_gain_b, grad_shift_b)
    return (grad_below, grads)

def reference(hidden_in, segment_ids, grad_out, qkv_weight, qv_bias, proj_weight, proj_bias, first_gain, first_shift, up_weight, up_bias, down_weight, down_bias, second_gain, second_shift):
    stacked = (qkv_weight, qv_bias, proj_weight, proj_bias, first_gain, first_shift, up_weight, up_bias, down_weight, down_bias, second_gain, second_shift)

    def one_sequence(totals, inputs):
        tokens_low, seg_ids, cotangent = inputs
        lowered = tokens_low
        resid = tokens_low.astype(jnp.float32)
        records = []
        for layer_number in range(LAYERS):
            params = tuple((array[layer_number] for array in stacked))
            record, resid = layer_forward(lowered, resid, seg_ids, params)
            records.append(record)
            lowered = rounded(resid)
        upstream = cotangent.astype(jnp.float32)
        new_totals = list(totals)
        for layer_number in reversed(range(LAYERS)):
            params = tuple((array[layer_number] for array in stacked))
            upstream, grads = layer_backward(records[layer_number], upstream, seg_ids, params)
            new_totals[layer_number] = tuple((old + new for old, new in zip(totals[layer_number], grads)))
        return (tuple(new_totals), (resid, upstream))
    start = tuple((tuple((jnp.zeros(array.shape[1:], jnp.float32) for array in stacked)) for layer_number in range(LAYERS)))
    totals, (hidden_out, grad_in) = lax.scan(one_sequence, start, (hidden_in, segment_ids, grad_out))
    joined = [jnp.stack([totals[layer_number][index] for layer_number in range(LAYERS)]) for index in range(12)]
    return (hidden_out, grad_in, joined[0], joined[1], joined[2], joined[3], joined[4], joined[5], joined[6], joined[7], joined[8], joined[9], joined[10], joined[11])
```

```python
import math

import jax
import jax.numpy as jnp
from jax import lax
from jax.sharding import PartitionSpec as P

HEADS = 12
HEAD_DIM = 64
LAYERS = 1


def layer_norm(resid, gain, shift):
    center = resid - jnp.mean(resid, axis=-1, keepdims=True)
    variance = jnp.mean(center * center, axis=-1, keepdims=True)
    return center * lax.rsqrt(variance + 1e-12) * gain + shift


def gelu_value(before):
    return before * 0.5 * (1.0 + lax.erf(before * (1.0 / math.sqrt(2.0))))


def gelu_slope(before):
    cumulative = 0.5 * (1.0 + lax.erf(before * (1.0 / math.sqrt(2.0))))
    density = jnp.exp(-0.5 * before * before) * (1.0 / math.sqrt(2.0 * math.pi))
    return cumulative + before * density


def split_steps(axes):
    steps = []
    for axis in axes:
        bit = lax.axis_size(axis) // 2
        while bit:
            steps.append((axis, bit))
            bit //= 2
    return steps


def gather_order(axes, flipped):
    along = [step for step in split_steps(axes) if step[0] == "ctx" and step[1] > 1]
    plane = [step for step in split_steps(axes) if step[0] == "dp"]
    pair = [step for step in split_steps(axes) if step == ("ctx", 1)]
    return along + (plane[::-1] if flipped else plane) + pair


def swap(array, step):
    axis, bit = step
    count = lax.axis_size(axis)
    return lax.ppermute(array, axis, [(index, index ^ bit) for index in range(count)])


def gather(shard, axes, flipped=False):
    rank = split_steps(axes)
    have = []
    held = shard
    for step in gather_order(axes, flipped):
        other = swap(held, step)
        upper = (lax.axis_index(step[0]) & step[1]) != 0
        low = jnp.where(upper, other, held)
        high = jnp.where(upper, held, other)
        have = sorted(have + [step], key=rank.index)
        held = jnp.stack([low, high], axis=have.index(step))
    return held.reshape((-1,) + shard.shape)


def scatter(parts, axes, flipped=False, sent=jnp.bfloat16):
    have = split_steps(axes)
    held = parts.reshape((2,) * len(have) + parts.shape[1:])
    for step in gather_order(axes, flipped)[::-1]:
        place = have.index(step)
        upper = ((lax.axis_index(step[0]) & step[1]) != 0).astype(jnp.int32)
        keep = lax.dynamic_index_in_dim(held, upper, place, keepdims=False)
        send = lax.dynamic_index_in_dim(held, 1 - upper, place, keepdims=False)
        other = swap(send.astype(sent), step)
        held = keep.astype(jnp.float32) + other.astype(jnp.float32)
        have.remove(step)
    return held


ALL = ("dp", "ctx")


def gather_weight(shard):
    half = shard.shape[1] // 2
    first = gather(shard[:, :half], ALL)
    second = gather(shard[:, half:], ALL, flipped=True)
    whole = jnp.concatenate([first, second], axis=2)
    return whole.reshape(-1, shard.shape[1])


def scatter_weight(grad):
    count = lax.axis_size("dp") * lax.axis_size("ctx")
    width = grad.shape[1]
    parts = grad.astype(jnp.bfloat16).reshape(count, -1, width)
    half = width // 2
    first = scatter(parts[:, :, :half], ALL)
    second = scatter(parts[:, :, half:], ALL, flipped=True)
    return jnp.concatenate([first, second], axis=1)


SMALL = (1, 3, 4, 5, 7, 9, 10, 11)


def gather_small(shards):
    lengths = [shard.shape[0] for shard in shards]
    whole = gather(jnp.concatenate(shards)[None], ALL)[:, 0]
    out, at = [], 0
    for length in lengths:
        out.append(whole[:, at : at + length].reshape(-1))
        at += length
    return out


def scatter_small(grads):
    count = lax.axis_size("dp") * lax.axis_size("ctx")
    rows = [grad.reshape(count, 1, -1) for grad in grads]
    own = scatter(jnp.concatenate(rows, axis=2), ALL, sent=jnp.float32)[0]
    out, at = [], 0
    for row in rows:
        out.append(own[at : at + row.shape[2]])
        at += row.shape[2]
    return out


def fetch_forward(stacked, layer_number):
    shards = [array[layer_number] for array in stacked]
    params = [None] * 12
    width = shards[0].shape[1]
    joint = gather_weight(jnp.concatenate([shards[0], shards[2]], axis=1))
    params[0], params[2] = joint[:, :width], joint[:, width:]
    small = gather_small([shards[index] for index in SMALL])
    for index, value in zip(SMALL, small):
        params[index] = value
    params[6] = gather_weight(shards[6])
    params[8] = gather_weight(shards[8])
    return tuple(params)


def gather_rows(local):
    seq_count, span = local.shape[:2]
    whole = jnp.moveaxis(gather(local, ("ctx",)), 0, 1)
    return whole.reshape((seq_count, -1) + local.shape[2:])


def scatter_rows(parts):
    seq_count, positions, width = parts.shape
    count = lax.axis_size("ctx")
    blocks = parts.reshape(seq_count, count, positions // count, width)
    return scatter(jnp.moveaxis(blocks, 1, 0), ("ctx",))


def scores_of(query_rows, whole_keys, seg_local, seg_whole):
    seq_count = query_rows.shape[0]
    key_all = whole_keys.reshape(seq_count, -1, HEADS, HEAD_DIM)
    logits = jnp.einsum("bqhd,bkhd->bhqk", query_rows, key_all, preferred_element_type=jnp.float32)
    logits = logits * (1.0 / math.sqrt(HEAD_DIM))
    same = seg_local[:, None, :, None] == seg_whole[:, None, None, :]
    return jnp.where(same, logits, -1e30)


def attend_forward(query_rows, whole, seg_local):
    whole_keys, whole_values, seg_whole = whole
    seq_count = query_rows.shape[0]
    scores = scores_of(query_rows, whole_keys, seg_local, seg_whole)
    log_total = jnp.log(jnp.sum(jnp.exp(scores), axis=-1, keepdims=True))
    attn_weights = jnp.exp(scores - log_total).astype(jnp.bfloat16)
    value_all = whole_values.reshape(seq_count, -1, HEADS, HEAD_DIM)
    mixed = jnp.einsum(
        "bhqk,bkhd->bqhd", attn_weights, value_all, preferred_element_type=jnp.float32
    )
    return (mixed.astype(jnp.bfloat16), attn_weights)


def layer_forward(lowered, resid, seg_local, params):
    qkv_w, qv_b, proj_w, proj_b, gain_a, shift_a, up_w, up_b, down_w, down_b, gain_b, shift_b = (
        params
    )
    width = qkv_w.shape[0]
    seq_count, span = seg_local.shape
    mixed_in = jnp.dot(lowered, qkv_w, preferred_element_type=jnp.float32)
    query_rows = (
        (mixed_in[:, :width] + qv_b[:width].astype(jnp.float32))
        .astype(jnp.bfloat16)
        .reshape(seq_count, span, HEADS, HEAD_DIM)
    )
    key_rows = mixed_in[:, width : 2 * width].astype(jnp.bfloat16).reshape(seq_count, span, width)
    value_rows = (
        (mixed_in[:, 2 * width :] + qv_b[width:].astype(jnp.float32))
        .astype(jnp.bfloat16)
        .reshape(seq_count, span, width)
    )
    pairs = gather_rows(jnp.concatenate([key_rows, value_rows], axis=2))
    whole = (pairs[:, :, :width], pairs[:, :, width:], gather_rows(seg_local))
    mixed, attn_weights = attend_forward(query_rows, whole, seg_local)
    context = mixed.reshape(-1, width)
    first_sum = (
        resid
        + jnp.dot(context, proj_w, preferred_element_type=jnp.float32)
        + proj_b.astype(jnp.float32)
    )
    normed = layer_norm(first_sum, gain_a.astype(jnp.float32), shift_a.astype(jnp.float32))
    normed_low = normed.astype(jnp.bfloat16)
    before = jnp.dot(normed_low, up_w, preferred_element_type=jnp.float32) + up_b.astype(
        jnp.float32
    )
    activated = gelu_value(before).astype(jnp.bfloat16)
    second_sum = (
        normed
        + jnp.dot(activated, down_w, preferred_element_type=jnp.float32)
        + down_b.astype(jnp.float32)
    )
    result = layer_norm(second_sum, gain_b.astype(jnp.float32), shift_b.astype(jnp.float32))
    record = (
        lowered,
        query_rows,
        whole,
        attn_weights,
        context,
        first_sum,
        normed_low,
        before,
        activated,
        second_sum,
    )
    return (record, result)


def layer_backward(record, upstream, seg_local, params):
    qkv_w, qv_b, proj_w, proj_b, gain_a, shift_a, up_w, up_b, down_w, down_b, gain_b, shift_b = (
        params
    )
    (
        lowered,
        query_rows,
        whole,
        attn_weights,
        context,
        first_sum,
        normed_low,
        before,
        activated,
        second_sum,
    ) = record
    width = qkv_w.shape[0]
    seq_count, span = seg_local.shape
    unused, second_back = jax.vjp(
        layer_norm, second_sum, gain_b.astype(jnp.float32), shift_b.astype(jnp.float32)
    )
    grad_second, grad_gain_b, grad_shift_b = second_back(upstream)
    grad_second_low = grad_second.astype(jnp.bfloat16)
    grad_down_w = jnp.dot(activated.T, grad_second_low, preferred_element_type=jnp.float32)
    grad_down_b = jnp.sum(grad_second, axis=0)
    grad_before = jnp.dot(
        grad_second_low, down_w.T, preferred_element_type=jnp.float32
    ) * gelu_slope(before)
    grad_up_b = jnp.sum(grad_before, axis=0)
    grad_before_low = grad_before.astype(jnp.bfloat16)
    grad_up_w = jnp.dot(normed_low.T, grad_before_low, preferred_element_type=jnp.float32)
    grad_normed = grad_second + jnp.dot(grad_before_low, up_w.T, preferred_element_type=jnp.float32)
    unused_two, first_back = jax.vjp(
        layer_norm, first_sum, gain_a.astype(jnp.float32), shift_a.astype(jnp.float32)
    )
    grad_first, grad_gain_a, grad_shift_a = first_back(grad_normed)
    grad_first_low = grad_first.astype(jnp.bfloat16)
    grad_proj_w = jnp.dot(context.T, grad_first_low, preferred_element_type=jnp.float32)
    grad_proj_b = jnp.sum(grad_first, axis=0)
    grad_context = jnp.dot(grad_first_low, proj_w.T, preferred_element_type=jnp.float32).astype(
        jnp.bfloat16
    )
    grad_context = grad_context.reshape(seq_count, span, HEADS, HEAD_DIM)
    whole_keys, whole_values, unused_three = whole
    value_all = whole_values.reshape(seq_count, -1, HEADS, HEAD_DIM)
    key_all = whole_keys.reshape(seq_count, -1, HEADS, HEAD_DIM)
    grad_weights = jnp.einsum(
        "bqhd,bkhd->bhqk", grad_context, value_all, preferred_element_type=jnp.float32
    )
    inner = jnp.sum(attn_weights.astype(jnp.float32) * grad_weights, axis=-1, keepdims=True)
    grad_scores = (
        attn_weights.astype(jnp.float32) * (grad_weights - inner) * (1.0 / math.sqrt(HEAD_DIM))
    ).astype(jnp.bfloat16)
    grad_query = jnp.einsum(
        "bhqk,bkhd->bqhd", grad_scores, key_all, preferred_element_type=jnp.float32
    ).reshape(-1, width)
    key_part = jnp.einsum(
        "bhqk,bqhd->bkhd", grad_scores, query_rows, preferred_element_type=jnp.float32
    ).reshape(seq_count, -1, width)
    value_part = jnp.einsum(
        "bhqk,bqhd->bkhd", attn_weights, grad_context, preferred_element_type=jnp.float32
    ).reshape(seq_count, -1, width)
    grad_qv_b = jnp.concatenate([jnp.sum(grad_query, axis=0), jnp.sum(value_part, axis=(0, 1))])
    owned = scatter_rows(jnp.concatenate([key_part, value_part], axis=2).astype(jnp.bfloat16))
    grad_key = owned[:, :, :width].reshape(-1, width)
    grad_value = owned[:, :, width:].reshape(-1, width)
    grad_qkv = jnp.concatenate([grad_query, grad_key, grad_value], axis=1).astype(jnp.bfloat16)
    grad_qkv_w = jnp.dot(lowered.T, grad_qkv, preferred_element_type=jnp.float32)
    grad_below = grad_first + jnp.dot(grad_qkv, qkv_w.T, preferred_element_type=jnp.float32)
    grads = (
        grad_qkv_w,
        grad_qv_b,
        grad_proj_w,
        grad_proj_b,
        grad_gain_a,
        grad_shift_a,
        grad_up_w,
        grad_up_b,
        grad_down_w,
        grad_down_b,
        grad_gain_b,
        grad_shift_b,
    )
    return (grad_below, grads)


def on_device(
    hidden_in,
    segment_ids,
    grad_out,
    qkv_weight,
    qv_bias,
    proj_weight,
    proj_bias,
    first_gain,
    first_shift,
    up_weight,
    up_bias,
    down_weight,
    down_bias,
    second_gain,
    second_shift,
):
    stacked = (
        qkv_weight,
        qv_bias,
        proj_weight,
        proj_bias,
        first_gain,
        first_shift,
        up_weight,
        up_bias,
        down_weight,
        down_bias,
        second_gain,
        second_shift,
    )
    seq_count, span, width = hidden_in.shape
    lowered = hidden_in.reshape(-1, width)
    resid = lowered.astype(jnp.float32)
    layer_number = 0
    params = fetch_forward(stacked, layer_number)
    fetched = [params]
    record, resid = layer_forward(lowered, resid, segment_ids, params)
    records = [record]
    hidden_out = resid.reshape(seq_count, span, width)
    upstream = grad_out.reshape(-1, width)
    collected = [None] * LAYERS
    for layer_number in reversed(range(LAYERS)):
        params = fetched[layer_number]
        upstream, local_grads = layer_backward(records[layer_number], upstream, segment_ids, params)
        owned = [None] * 12
        for index in (8, 6, 2, 0):
            owned[index] = scatter_weight(local_grads[index])
        small = scatter_small([local_grads[index] for index in SMALL])
        for index, value in zip(SMALL, small):
            owned[index] = value
        collected[layer_number] = tuple(owned)
    joined = [jnp.stack([collected[0][index]]) for index in range(12)]
    grad_in = upstream.reshape(seq_count, span, width)
    return (
        hidden_out,
        grad_in,
        joined[0],
        joined[1],
        joined[2],
        joined[3],
        joined[4],
        joined[5],
        joined[6],
        joined[7],
        joined[8],
        joined[9],
        joined[10],
        joined[11],
    )


def solution(mesh):
    in_specs = (
        P("dp", "ctx", None),
        P("dp", "ctx"),
        P("dp", "ctx", None),
        P(None, ("dp", "ctx"), None),
        P(None, ("dp", "ctx")),
        P(None, ("dp", "ctx"), None),
        P(None, ("dp", "ctx")),
        P(None, ("dp", "ctx")),
        P(None, ("dp", "ctx")),
        P(None, ("dp", "ctx"), None),
        P(None, ("dp", "ctx")),
        P(None, ("dp", "ctx"), None),
        P(None, ("dp", "ctx")),
        P(None, ("dp", "ctx")),
        P(None, ("dp", "ctx")),
    )
    out_specs = (
        P("dp", "ctx", None),
        P("dp", "ctx", None),
        P(None, ("dp", "ctx"), None),
        P(None, ("dp", "ctx")),
        P(None, ("dp", "ctx"), None),
        P(None, ("dp", "ctx")),
        P(None, ("dp", "ctx")),
        P(None, ("dp", "ctx")),
        P(None, ("dp", "ctx"), None),
        P(None, ("dp", "ctx")),
        P(None, ("dp", "ctx"), None),
        P(None, ("dp", "ctx")),
        P(None, ("dp", "ctx")),
        P(None, ("dp", "ctx")),
    )
    return jax.shard_map(
        on_device, mesh=mesh, in_specs=in_specs, out_specs=out_specs, check_vma=False
    )
```

```python
import math

import jax
import jax.numpy as jnp
from jax import lax
from jax.sharding import PartitionSpec as P

HEADS = 12
HEAD_DIM = 64
LAYERS = 1


def layer_norm(resid, gain, shift):
    center = resid - jnp.mean(resid, axis=-1, keepdims=True)
    variance = jnp.mean(center * center, axis=-1, keepdims=True)
    return center * lax.rsqrt(variance + 1e-12) * gain + shift


def gelu_value(before):
    return before * 0.5 * (1.0 + lax.erf(before * (1.0 / math.sqrt(2.0))))


def gelu_slope(before):
    cumulative = 0.5 * (1.0 + lax.erf(before * (1.0 / math.sqrt(2.0))))
    density = jnp.exp(-0.5 * before * before) * (1.0 / math.sqrt(2.0 * math.pi))
    return cumulative + before * density


def split_steps(axes):
    steps = []
    for axis in axes:
        bit = lax.axis_size(axis) // 2
        while bit:
            steps.append((axis, bit))
            bit //= 2
    return steps


def gather_order(axes, flipped):
    along = [step for step in split_steps(axes) if step[0] == "ctx" and step[1] > 1]
    plane = [step for step in split_steps(axes) if step[0] == "dp"]
    pair = [step for step in split_steps(axes) if step == ("ctx", 1)]
    return along + (plane[::-1] if flipped else plane) + pair


def swap(array, step):
    axis, bit = step
    count = lax.axis_size(axis)
    return lax.ppermute(array, axis, [(index, index ^ bit) for index in range(count)])


def gather(shard, axes, flipped=False):
    rank = split_steps(axes)
    have = []
    held = shard
    for step in gather_order(axes, flipped):
        other = swap(held, step)
        upper = (lax.axis_index(step[0]) & step[1]) != 0
        low = jnp.where(upper, other, held)
        high = jnp.where(upper, held, other)
        have = sorted(have + [step], key=rank.index)
        held = jnp.stack([low, high], axis=have.index(step))
    return held.reshape((-1,) + shard.shape)


class Sum:
    def __init__(self, parts, axes, flipped=False, sent=jnp.bfloat16):
        self.have = split_steps(axes)
        self.left = gather_order(axes, flipped)[::-1]
        self.sent = sent
        self.held = parts.reshape((2,) * len(self.have) + parts.shape[1:])

    def advance(self, steps):
        for step in self.left[:steps]:
            place = self.have.index(step)
            upper = ((lax.axis_index(step[0]) & step[1]) != 0).astype(jnp.int32)
            keep = lax.dynamic_index_in_dim(self.held, upper, place, keepdims=False)
            send = lax.dynamic_index_in_dim(self.held, 1 - upper, place, keepdims=False)
            other = swap(send.astype(self.sent), step)
            self.held = keep.astype(jnp.float32) + other.astype(jnp.float32)
            self.have.remove(step)
        self.left = self.left[steps:]

    def result(self):
        self.advance(len(self.left))
        return self.held


def scatter(parts, axes, sent=jnp.bfloat16):
    return Sum(parts, axes, sent=sent).result()


ALL = ("dp", "ctx")


def gather_weight(shard):
    half = shard.shape[1] // 2
    first = gather(shard[:, :half], ALL)
    second = gather(shard[:, half:], ALL, flipped=True)
    whole = jnp.concatenate([first, second], axis=2)
    return whole.reshape(-1, shard.shape[1])


class WeightSum:
    def __init__(self, grad):
        count = lax.axis_size("dp") * lax.axis_size("ctx")
        width = grad.shape[1]
        parts = grad.astype(jnp.bfloat16).reshape(count, -1, width)
        half = width // 2
        self.halves = (
            Sum(parts[:, :, :half], ALL),
            Sum(parts[:, :, half:], ALL, flipped=True),
        )

    def advance(self, steps):
        for half in self.halves:
            half.advance(steps)

    def result(self):
        return jnp.concatenate([half.result() for half in self.halves], axis=1)


def after(value, *sums):
    halves = [half for each in sums for half in each.halves]
    value, held = lax.optimization_barrier((value, [half.held for half in halves]))
    for half, array in zip(halves, held):
        half.held = array
    return value


SMALL = (1, 3, 4, 5, 7, 9, 10, 11)


def gather_small(shards):
    lengths = [shard.shape[0] for shard in shards]
    whole = gather(jnp.concatenate(shards)[None], ALL)[:, 0]
    out, at = [], 0
    for length in lengths:
        out.append(whole[:, at : at + length].reshape(-1))
        at += length
    return out


def scatter_small(grads):
    count = lax.axis_size("dp") * lax.axis_size("ctx")
    rows = [grad.reshape(count, 1, -1) for grad in grads]
    own = scatter(jnp.concatenate(rows, axis=2), ALL, sent=jnp.float32)[0]
    out, at = [], 0
    for row in rows:
        out.append(own[at : at + row.shape[2]])
        at += row.shape[2]
    return out


def fetch_forward(stacked, layer_number):
    shards = [array[layer_number] for array in stacked]
    params = [None] * 12
    params[0] = gather_weight(shards[0])
    small = gather_small([shards[index] for index in SMALL])
    for index, value in zip(SMALL, small):
        params[index] = value
    params[0], shards[2], shards[6], shards[8] = lax.optimization_barrier(
        (params[0], shards[2], shards[6], shards[8])
    )
    params[2] = gather_weight(shards[2])
    params[6] = gather_weight(shards[6])
    params[8] = gather_weight(shards[8])
    return tuple(params)


def gather_rows(local):
    seq_count, span = local.shape[:2]
    whole = jnp.moveaxis(gather(local, ("ctx",)), 0, 1)
    return whole.reshape((seq_count, -1) + local.shape[2:])


def scatter_rows(parts):
    seq_count, positions, width = parts.shape
    count = lax.axis_size("ctx")
    blocks = parts.reshape(seq_count, count, positions // count, width)
    return scatter(jnp.moveaxis(blocks, 1, 0), ("ctx",))


def scores_of(query_rows, whole_keys, seg_local, seg_whole):
    seq_count = query_rows.shape[0]
    key_all = whole_keys.reshape(seq_count, -1, HEADS, HEAD_DIM)
    logits = jnp.einsum("bqhd,bkhd->bhqk", query_rows, key_all, preferred_element_type=jnp.float32)
    logits = logits * (1.0 / math.sqrt(HEAD_DIM))
    same = seg_local[:, None, :, None] == seg_whole[:, None, None, :]
    return jnp.where(same, logits, -1e30)


def attend_forward(query_rows, whole, seg_local):
    whole_keys, whole_values, seg_whole = whole
    seq_count = query_rows.shape[0]
    scores = scores_of(query_rows, whole_keys, seg_local, seg_whole)
    log_total = jnp.log(jnp.sum(jnp.exp(scores), axis=-1, keepdims=True))
    attn_weights = jnp.exp(scores - log_total).astype(jnp.bfloat16)
    value_all = whole_values.reshape(seq_count, -1, HEADS, HEAD_DIM)
    mixed = jnp.einsum(
        "bhqk,bkhd->bqhd", attn_weights, value_all, preferred_element_type=jnp.float32
    )
    return (mixed.astype(jnp.bfloat16), attn_weights)


def layer_forward(lowered, resid, seg_local, params):
    qkv_w, qv_b, proj_w, proj_b, gain_a, shift_a, up_w, up_b, down_w, down_b, gain_b, shift_b = (
        params
    )
    width = qkv_w.shape[0]
    seq_count, span = seg_local.shape
    mixed_in = jnp.dot(lowered, qkv_w, preferred_element_type=jnp.float32)
    query_rows = (
        (mixed_in[:, :width] + qv_b[:width].astype(jnp.float32))
        .astype(jnp.bfloat16)
        .reshape(seq_count, span, HEADS, HEAD_DIM)
    )
    key_rows = mixed_in[:, width : 2 * width].astype(jnp.bfloat16).reshape(seq_count, span, width)
    value_rows = (
        (mixed_in[:, 2 * width :] + qv_b[width:].astype(jnp.float32))
        .astype(jnp.bfloat16)
        .reshape(seq_count, span, width)
    )
    pairs = gather_rows(jnp.concatenate([key_rows, value_rows], axis=2))
    whole = (pairs[:, :, :width], pairs[:, :, width:], gather_rows(seg_local))
    mixed, attn_weights = attend_forward(query_rows, whole, seg_local)
    context = mixed.reshape(-1, width)
    first_sum = (
        resid
        + jnp.dot(context, proj_w, preferred_element_type=jnp.float32)
        + proj_b.astype(jnp.float32)
    )
    normed = layer_norm(first_sum, gain_a.astype(jnp.float32), shift_a.astype(jnp.float32))
    normed_low = normed.astype(jnp.bfloat16)
    before = jnp.dot(normed_low, up_w, preferred_element_type=jnp.float32) + up_b.astype(
        jnp.float32
    )
    activated = gelu_value(before).astype(jnp.bfloat16)
    second_sum = (
        normed
        + jnp.dot(activated, down_w, preferred_element_type=jnp.float32)
        + down_b.astype(jnp.float32)
    )
    result = layer_norm(second_sum, gain_b.astype(jnp.float32), shift_b.astype(jnp.float32))
    record = (
        lowered,
        query_rows,
        whole,
        attn_weights,
        context,
        first_sum,
        normed_low,
        before,
        activated,
        second_sum,
    )
    return (record, result)


def layer_backward(record, upstream, seg_local, params):
    qkv_w, qv_b, proj_w, proj_b, gain_a, shift_a, up_w, up_b, down_w, down_b, gain_b, shift_b = (
        params
    )
    (
        lowered,
        query_rows,
        whole,
        attn_weights,
        context,
        first_sum,
        normed_low,
        before,
        activated,
        second_sum,
    ) = record
    width = qkv_w.shape[0]
    seq_count, span = seg_local.shape
    unused, second_back = jax.vjp(
        layer_norm, second_sum, gain_b.astype(jnp.float32), shift_b.astype(jnp.float32)
    )
    grad_second, grad_gain_b, grad_shift_b = second_back(upstream)
    grad_second_low = grad_second.astype(jnp.bfloat16)
    grad_down_w = jnp.dot(activated.T, grad_second_low, preferred_element_type=jnp.float32)
    down_sum = WeightSum(grad_down_w)
    down_sum.advance(1)
    grad_down_b = jnp.sum(grad_second, axis=0)
    grad_before = jnp.dot(
        grad_second_low, down_w.T, preferred_element_type=jnp.float32
    ) * gelu_slope(before)
    grad_up_b = jnp.sum(grad_before, axis=0)
    grad_before_low = grad_before.astype(jnp.bfloat16)
    grad_up_w = jnp.dot(normed_low.T, grad_before_low, preferred_element_type=jnp.float32)
    up_sum = WeightSum(grad_up_w)
    grad_normed = grad_second + jnp.dot(grad_before_low, up_w.T, preferred_element_type=jnp.float32)
    unused_two, first_back = jax.vjp(
        layer_norm, first_sum, gain_a.astype(jnp.float32), shift_a.astype(jnp.float32)
    )
    grad_first, grad_gain_a, grad_shift_a = first_back(grad_normed)
    grad_first_low = after(grad_first.astype(jnp.bfloat16), down_sum)
    down_sum.advance(1)
    up_sum.advance(1)
    grad_proj_w = jnp.dot(context.T, grad_first_low, preferred_element_type=jnp.float32)
    proj_sum = WeightSum(grad_proj_w)
    grad_proj_b = jnp.sum(grad_first, axis=0)
    grad_context = jnp.dot(grad_first_low, proj_w.T, preferred_element_type=jnp.float32).astype(
        jnp.bfloat16
    )
    grad_context = after(grad_context, up_sum)
    grad_context = grad_context.reshape(seq_count, span, HEADS, HEAD_DIM)
    whole_keys, whole_values, unused_three = whole
    value_all = whole_values.reshape(seq_count, -1, HEADS, HEAD_DIM)
    key_all = whole_keys.reshape(seq_count, -1, HEADS, HEAD_DIM)
    grad_weights = jnp.einsum(
        "bqhd,bkhd->bhqk", grad_context, value_all, preferred_element_type=jnp.float32
    )
    inner = jnp.sum(attn_weights.astype(jnp.float32) * grad_weights, axis=-1, keepdims=True)
    grad_scores = (
        attn_weights.astype(jnp.float32) * (grad_weights - inner) * (1.0 / math.sqrt(HEAD_DIM))
    ).astype(jnp.bfloat16)
    grad_scores = after(grad_scores, down_sum)
    down_sum.advance(1)
    up_sum.advance(1)
    proj_sum.advance(1)
    grad_query = jnp.einsum(
        "bhqk,bkhd->bqhd", grad_scores, key_all, preferred_element_type=jnp.float32
    ).reshape(-1, width)
    key_part = jnp.einsum(
        "bhqk,bqhd->bkhd", grad_scores, query_rows, preferred_element_type=jnp.float32
    ).reshape(seq_count, -1, width)
    value_part = jnp.einsum(
        "bhqk,bqhd->bkhd", attn_weights, grad_context, preferred_element_type=jnp.float32
    ).reshape(seq_count, -1, width)
    grad_qv_b = jnp.concatenate([jnp.sum(grad_query, axis=0), jnp.sum(value_part, axis=(0, 1))])
    parts = jnp.concatenate([key_part, value_part], axis=2).astype(jnp.bfloat16)
    parts = after(parts, down_sum, up_sum, proj_sum)
    down_sum.advance(1)
    up_sum.advance(1)
    proj_sum.advance(2)
    owned = scatter_rows(parts)
    owned = after(owned, down_sum, up_sum, proj_sum)
    grad_key = owned[:, :, :width].reshape(-1, width)
    grad_value = owned[:, :, width:].reshape(-1, width)
    grad_qkv = jnp.concatenate([grad_query, grad_key, grad_value], axis=1).astype(jnp.bfloat16)
    grad_qkv_w = jnp.dot(lowered.T, grad_qkv, preferred_element_type=jnp.float32)
    grad_below = grad_first + jnp.dot(grad_qkv, qkv_w.T, preferred_element_type=jnp.float32)
    grads = (
        WeightSum(grad_qkv_w),
        grad_qv_b,
        proj_sum,
        grad_proj_b,
        grad_gain_a,
        grad_shift_a,
        up_sum,
        grad_up_b,
        down_sum,
        grad_down_b,
        grad_gain_b,
        grad_shift_b,
    )
    return (grad_below, grads)


def on_device(
    hidden_in,
    segment_ids,
    grad_out,
    qkv_weight,
    qv_bias,
    proj_weight,
    proj_bias,
    first_gain,
    first_shift,
    up_weight,
    up_bias,
    down_weight,
    down_bias,
    second_gain,
    second_shift,
):
    stacked = (
        qkv_weight,
        qv_bias,
        proj_weight,
        proj_bias,
        first_gain,
        first_shift,
        up_weight,
        up_bias,
        down_weight,
        down_bias,
        second_gain,
        second_shift,
    )
    seq_count, span, width = hidden_in.shape
    lowered = hidden_in.reshape(-1, width)
    resid = lowered.astype(jnp.float32)
    layer_number = 0
    params = fetch_forward(stacked, layer_number)
    fetched = [params]
    record, resid = layer_forward(lowered, resid, segment_ids, params)
    records = [record]
    hidden_out = resid.reshape(seq_count, span, width)
    upstream = grad_out.reshape(-1, width)
    collected = [None] * LAYERS
    for layer_number in reversed(range(LAYERS)):
        params = fetched[layer_number]
        upstream, local_grads = layer_backward(records[layer_number], upstream, segment_ids, params)
        owned = [None] * 12
        for index in (8, 6, 2, 0):
            owned[index] = local_grads[index].result()
        small = scatter_small([local_grads[index] for index in SMALL])
        for index, value in zip(SMALL, small):
            owned[index] = value
        collected[layer_number] = tuple(owned)
    joined = [jnp.stack([collected[0][index]]) for index in range(12)]
    grad_in = upstream.reshape(seq_count, span, width)
    return (
        hidden_out,
        grad_in,
        joined[0],
        joined[1],
        joined[2],
        joined[3],
        joined[4],
        joined[5],
        joined[6],
        joined[7],
        joined[8],
        joined[9],
        joined[10],
        joined[11],
    )


def solution(mesh):
    in_specs = (
        P("dp", "ctx", None),
        P("dp", "ctx"),
        P("dp", "ctx", None),
        P(None, ("dp", "ctx"), None),
        P(None, ("dp", "ctx")),
        P(None, ("dp", "ctx"), None),
        P(None, ("dp", "ctx")),
        P(None, ("dp", "ctx")),
        P(None, ("dp", "ctx")),
        P(None, ("dp", "ctx"), None),
        P(None, ("dp", "ctx")),
        P(None, ("dp", "ctx"), None),
        P(None, ("dp", "ctx")),
        P(None, ("dp", "ctx")),
        P(None, ("dp", "ctx")),
    )
    out_specs = (
        P("dp", "ctx", None),
        P("dp", "ctx", None),
        P(None, ("dp", "ctx"), None),
        P(None, ("dp", "ctx")),
        P(None, ("dp", "ctx"), None),
        P(None, ("dp", "ctx")),
        P(None, ("dp", "ctx")),
        P(None, ("dp", "ctx")),
        P(None, ("dp", "ctx"), None),
        P(None, ("dp", "ctx")),
        P(None, ("dp", "ctx"), None),
        P(None, ("dp", "ctx")),
        P(None, ("dp", "ctx")),
        P(None, ("dp", "ctx")),
    )
    return jax.shard_map(
        on_device, mesh=mesh, in_specs=in_specs, out_specs=out_specs, check_vma=False
    )
```
